32 devices in a mesh: frame: 8 (over y, x, core), module: 4 (over z).
Axes of the slice: x: 2, y: 2, z: 4, core: 2. Of those that a mesh axis runs over, the one named last changes fastest.
Arguments:
- raw_frames: int32 [2048, 32768], P('frame', 'module'), may hold values from 256 to 3856
- dark_frame: float32 [32768], P('module'), may hold values from 0 to 240
- flat_field: float32 [32768], P('module'), may hold values from 0.125 to 2.625, as said below
- membership: int32 [16, 32768], P(None, 'module'), may hold values from 0 to 1, as said below
Outputs:
- correlation: float32 [16, 8, 5, 256, 256], P('module', 'frame')
The draws below stay inside these ranges and needn't reach their ends.
Inputs may be any that keep to these rules, and one draw needn't show every extreme that they name: `membership`: each pixel belongs to exactly one q-bin, and every module holds exactly 512 pixels of each q-bin, in no particular order. `flat_field`: positive gains.
All inputs are finite; a program needn't handle non-finite values.
Results may differ from the reference program's by a relative error of at most 0.0003.
Values may be sent and summed in bfloat16 or wider, within the bound.
A program may use at most 128 MiB of HBM per device.

```python
import jax
import jax.numpy as jnp
from jax import lax

BLK = 256
QBINS = 16
PIX_DEV = 8192
BLOCKS = 8
FRAMES = 2048
PIXELS = 32768


def bin_labels(key):
    modules = PIXELS // PIX_DEV
    per_bin = PIX_DEV // QBINS
    base_labels = jnp.tile(jnp.arange(PIX_DEV, dtype=jnp.int32) // per_bin, (modules, 1))
    shuffled = jax.random.permutation(jax.random.fold_in(key, 101), base_labels, axis=1, independent=True)
    return shuffled.reshape(PIXELS)


def draw_membership(key, part):
    labels = bin_labels(key)
    return (labels[None, :] == jnp.arange(QBINS, dtype=jnp.int32)[:, None]).astype(jnp.int32)


def draw_flat_field(key, part):
    gain_values = jax.random.uniform(key, (PIXELS,), jnp.float32, 0.25, 1.75)
    return gain_values


def draw_raw_frames(key, part):
    labels = bin_labels(key)
    modules = PIXELS // PIX_DEV
    keys = jax.random.split(jax.random.fold_in(key, 202), 7)
    octave_steps = jax.random.randint(keys[0], (QBINS,), 0, 21)
    window_base = 24 * jnp.left_shift(jnp.ones_like(octave_steps), octave_steps // 4) * (4 + octave_steps % 4) // 4
    window_phase = jax.random.randint(keys[1], (QBINS,), 0, 2)
    block_index = jnp.arange(FRAMES, dtype=jnp.int32) // BLK
    window = window_base[None, :] * (1 + (block_index[:, None] + window_phase[None, :]) % 2)
    frame_stop = jnp.arange(1, FRAMES + 1, dtype=jnp.int32)[:, None]

    def one_module(module):
        module_keys = jax.random.split(jax.random.fold_in(keys[2], module), 3)
        local_labels = lax.dynamic_slice_in_dim(labels, module * PIX_DEV, PIX_DEV)
        local_window = jnp.take(window, local_labels, axis=1)
        window_start = jnp.maximum(frame_stop - local_window, 0)
        fields = []
        for field_key in (module_keys[0], module_keys[1]):
            increments = jax.random.randint(field_key, (FRAMES, PIX_DEV), -15, 16)
            totals = jnp.concatenate([jnp.zeros((1, PIX_DEV), jnp.int32), jnp.cumsum(increments, axis=0, dtype=jnp.int32)], axis=0)
            fields.append(totals[1:] - jnp.take_along_axis(totals, window_start, axis=0))
        divisor = jnp.maximum(160 * local_window // 200, 1)
        speckle = jnp.minimum((fields[0] * fields[0] + fields[1] * fields[1]) // divisor, 836)
        shot_noise = jax.random.randint(module_keys[2], (FRAMES, PIX_DEV), 0, 64)
        level_counts = (speckle + shot_noise) * (modules - 1 + 3 * module) // (modules - 1)
        return 256 + level_counts
    stacked = lax.map(one_module, jnp.arange(modules, dtype=jnp.int32))
    frame_counts = jnp.transpose(stacked, (1, 0, 2)).reshape(FRAMES, PIXELS)
    high_row = jax.random.randint(keys[3], (), 0, FRAMES)
    high_column = jax.random.randint(keys[4], (), 0, PIXELS)
    low_row = (high_row + 1 + jax.random.randint(keys[5], (), 0, FRAMES - 1)) % FRAMES
    low_column = jax.random.randint(keys[6], (), 0, PIXELS)
    frame_counts = frame_counts.at[high_row, high_column].set(3856)
    frame_counts = frame_counts.at[low_row, low_column].set(256)
    return frame_counts.astype(jnp.int32)


def level_of(own_key, shape, pieces, least, largest):
    level = 1.0
    for dim, shards_of in pieces:
        steps = jax.random.uniform(jax.random.fold_in(jax.random.fold_in(own_key, 6), dim), (shards_of,), jnp.float32, least / len(pieces), largest / len(pieces))
        level = level * jnp.repeat(jnp.exp(steps), shape[dim] // shards_of).reshape((-1,) + (1,) * (len(shape) - 1 - dim))
    return level


def setup_inputs(seed: int = 0) -> dict:
    key_of = jax.random.split(jax.random.key(seed), 5)
    return {
        "raw_frames": draw_raw_frames(jax.random.fold_in(key_of[4], 71), 0),
        "dark_frame": jnp.clip(240.0 * jax.random.uniform(key_of[1], (PIXELS,), jnp.float32) ** level_of(key_of[1], (PIXELS,), ((0, 4),), -0.2, 0.2), 0.0, 240.0),
        "flat_field": draw_flat_field(jax.random.fold_in(key_of[4], 71), 0),
        "membership": draw_membership(jax.random.fold_in(key_of[4], 71), 0),
    }


def reference(raw_frames, dark_frame, flat_field, membership):
    intensity = (raw_frames.astype(jnp.float32) - dark_frame[None, :]) * flat_field[None, :]
    members = membership.astype(jnp.float32)
    bin_sums = jnp.dot(intensity, members.T, precision=lax.Precision.HIGHEST)
    counts = lax.optimization_barrier(jnp.sum(members, axis=1))
    scales = jnp.sqrt(counts)[None, :] / bin_sums
    pixel_scale = jnp.dot(scales, members, precision=lax.Precision.HIGHEST)
    scaled = (intensity * pixel_scale).astype(jnp.bfloat16)
    labels = lax.optimization_barrier(jnp.sum(membership * jnp.arange(QBINS, dtype=jnp.int32)[:, None], axis=0)).astype(jnp.int32)
    ordering = jnp.argsort(labels, stable=True)
    per_bin = PIXELS // QBINS
    grouped = jnp.take(scaled, ordering, axis=1).reshape(BLOCKS, BLK, QBINS, per_bin)
    zero_blocks = jnp.zeros((2, BLK, QBINS, per_bin), jnp.bfloat16)
    padded = jnp.concatenate([grouped, zero_blocks], axis=0)

    def single_block(block_index):
        target = lax.dynamic_index_in_dim(grouped, block_index, 0, keepdims=False).astype(jnp.float32)
        partners = lax.dynamic_slice_in_dim(padded, block_index, 3, 0).astype(jnp.float32)
        return jnp.einsum('urp,jvrp->rjuv', target, partners, precision=lax.Precision.HIGHEST)
    forward = lax.map(single_block, jnp.arange(BLOCKS, dtype=jnp.int32))
    zero_one = jnp.zeros((1, QBINS, BLK, BLK), forward.dtype)
    zero_two = jnp.zeros((2, QBINS, BLK, BLK), forward.dtype)
    one_back = jnp.swapaxes(jnp.concatenate([zero_one, forward[:-1, :, 1]], axis=0), 2, 3)
    two_back = jnp.swapaxes(jnp.concatenate([zero_two, forward[:-2, :, 2]], axis=0), 2, 3)
    result = jnp.concatenate([two_back[:, :, None], one_back[:, :, None], forward], axis=2)
    return jnp.transpose(result, (1, 0, 2, 3, 4))
```

```python
import functools

import jax
import jax.numpy as jnp
from jax import lax
from jax.experimental import pallas as pl
from jax.experimental.pallas import tpu as pltpu
from jax.sharding import PartitionSpec as P

MESH = pl.DeviceIdType.MESH
VMEM_BYTES = 60 * 1024 * 1024


def group_kernel(per_bin, order, raw, dark, flat, grouped, sums, turned):
    step = pl.program_id(0)
    chunk = raw.shape[1]
    intensity = (raw[...].astype(jnp.float32) - dark[...]) * flat[...]
    turned[pl.ds(pl.multiple_of(step * chunk, chunk), chunk), :] = intensity.T

    @pl.when(step == pl.num_programs(0) - 1)
    def _():
        frames = turned.shape[1]
        lane = lax.broadcasted_iota(jnp.int32, (8, frames), 0)

        @pl.loop(0, grouped.shape[0])
        def _(label):
            base = label * per_bin

            def rows(group, total):
                first = pl.multiple_of(group * 8, 8)
                tile = jnp.broadcast_to(turned[pl.ds(order[base + first], 1), :], (8, frames))
                for row in range(1, 8):
                    line = turned[pl.ds(order[base + first + row], 1), :]
                    tile = jnp.where(lane == row, line, tile)
                grouped[label, pl.ds(first, 8), :] = tile
                return total + tile

            total = lax.fori_loop(0, per_bin // 8, rows, jnp.zeros((8, frames), jnp.float32), unroll=4)
            sums[pl.ds(label, 1), :] = jnp.sum(total, axis=0, keepdims=True)


def group_by_bin(order, raw_frames, dark_frame, flat_field, bins):
    frames, pixels = raw_frames.shape
    per_bin = pixels // bins
    chunk = per_bin
    return pl.pallas_call(
        functools.partial(group_kernel, per_bin),
        out_shape=(
            jax.ShapeDtypeStruct((bins, per_bin, frames), jnp.float32),
            jax.ShapeDtypeStruct((bins, frames), jnp.float32),
        ),
        grid_spec=pltpu.PrefetchScalarGridSpec(
            num_scalar_prefetch=1,
            grid=(pixels // chunk,),
            in_specs=[
                pl.BlockSpec((frames, chunk), lambda i, o: (0, i)),
                pl.BlockSpec((1, chunk), lambda i, o: (0, i)),
                pl.BlockSpec((1, chunk), lambda i, o: (0, i)),
            ],
            out_specs=(
                pl.BlockSpec((bins, per_bin, frames), lambda i, o: (0, 0, 0)),
                pl.BlockSpec((bins, frames), lambda i, o: (0, 0)),
            ),
            scratch_shapes=[pltpu.VMEM((pixels, frames), jnp.float32)],
        ),
        compiler_params=pltpu.CompilerParams(vmem_limit_bytes=VMEM_BYTES),
    )(order, raw_frames, dark_frame[None, :], flat_field[None, :])


def gram(left, right):
    return lax.dot_general(
        left, right, (((0,), (0,)), ((), ())), preferred_element_type=jnp.float32
    )


def correlate_kernel(
    blocks,
    modules,
    grouped,
    sums,
    out,
    all_sums,
    scaled,
    own,
    far,
    near,
    staged,
    sum_send,
    sum_recv,
    bin_send,
    bin_recv,
    frame_send,
    frame_recv,
    result_send,
    result_recv,
):
    me = lax.axis_index("frame")
    module = lax.axis_index("module")
    bins, per_bin, _ = grouped.shape
    owned = bins // modules
    even = lax.rem(me, 2) == 0
    odd = lax.rem(me, 2) == 1
    has_down = me >= 2
    has_up = me + 2 < blocks
    mate = me + 1 - 2 * lax.rem(me, 2)

    barrier = pltpu.get_barrier_semaphore()

    def greet(frame, mod):
        pl.semaphore_signal(barrier, inc=1, device_id=(frame, mod), device_id_type=MESH)

    for gap in range(1, modules):
        greet(me, lax.rem(module + gap, modules))
    greet(mate, module)

    @pl.when(has_down)
    def _():
        greet(me - 2, module)

    @pl.when(has_up)
    def _():
        greet(me + 2, module)

    peers = modules + has_down.astype(jnp.int32) + has_up.astype(jnp.int32)
    pl.semaphore_wait(barrier, peers)

    def sum_copy(gap):
        return pltpu.make_async_remote_copy(
            src_ref=sums,
            dst_ref=all_sums.at[module],
            send_sem=sum_send.at[gap - 1],
            recv_sem=sum_recv.at[gap - 1],
            device_id=(me, lax.rem(module + gap, modules)),
            device_id_type=MESH,
        )

    for gap in range(1, modules):
        sum_copy(gap).start()
    all_sums[module] = sums[...]
    for gap in range(1, modules):
        sum_copy(gap).wait()
    total = all_sums[0]
    for source in range(1, modules):
        total = total + all_sums[source]
    all_sums[0] = jnp.sqrt(jnp.float32(per_bin * modules)) / total

    def bin_copy(k, gap):
        owner = lax.rem(module + gap, modules)
        return pltpu.make_async_remote_copy(
            src_ref=scaled.at[owner * owned + k],
            dst_ref=own.at[k, pl.ds(pl.multiple_of(module * per_bin, per_bin), per_bin), :],
            send_sem=bin_send.at[k, gap - 1],
            recv_sem=bin_recv.at[k, gap - 1],
            device_id=(me, owner),
            device_id_type=MESH,
        )

    @pl.loop(0, owned)
    def _(k):
        for gap in range(1, modules):
            label = lax.rem(module + gap, modules) * owned + k
            factor = all_sums[0, pl.ds(label, 1), :]
            scaled[label] = (grouped[label] * factor).astype(jnp.bfloat16)
            bin_copy(k, gap).start()
        label = module * owned + k
        factor = all_sums[0, pl.ds(label, 1), :]
        own[k, pl.ds(pl.multiple_of(module * per_bin, per_bin), per_bin), :] = (
            grouped[label] * factor
        ).astype(jnp.bfloat16)

    def frame_copy(k, slot, target, frame):
        return pltpu.make_async_remote_copy(
            src_ref=own.at[k],
            dst_ref=target.at[k],
            send_sem=frame_send.at[slot, k],
            recv_sem=frame_recv.at[slot, k],
            device_id=(frame, module),
            device_id_type=MESH,
        )

    def down_copy(k):
        return frame_copy(k, 0, far, me - 2)

    def up_copy(k):
        return frame_copy(k, 0, far, me + 2)

    def mate_copy(k):
        return frame_copy(k, 1, near, mate)

    def result_copy(k, stage, place, frame):
        return pltpu.make_async_remote_copy(
            src_ref=staged.at[stage, k],
            dst_ref=out.at[k, place],
            send_sem=result_send.at[stage, k],
            recv_sem=result_recv.at[place, k],
            device_id=(frame, module),
            device_id_type=MESH,
        )

    def pass_on(k):
        for gap in range(1, modules):
            bin_copy(k, gap).wait()

        @pl.when(even & has_down)
        def _():
            down_copy(k).start()

        @pl.when(odd)
        def _():
            mate_copy(k).start()

        @pl.when(odd & has_up)
        def _():
            up_copy(k).start()

    def correlate(k):
        out[k, 2] = gram(own[k], own[k])

        @pl.when(even)
        def _():
            mate_copy(k).wait_recv()
            staged[0, k] = gram(near[k], own[k])
            result_copy(k, 0, 1, me + 1).start()
            out[k, 3] = gram(own[k], near[k])

        @pl.when(even & has_up)
        def _():
            up_copy(k).wait_recv()
            staged[1, k] = gram(far[k], own[k])
            result_copy(k, 1, 0, me + 2).start()
            staged[2, k] = gram(far[k], near[k])
            result_copy(k, 2, 1, me + 2).start()
            staged[3, k] = gram(near[k], far[k])
            result_copy(k, 3, 3, me + 1).start()
            out[k, 4] = gram(own[k], far[k])

        @pl.when(odd & has_down)
        def _():
            down_copy(k).wait_recv()
            staged[0, k] = gram(far[k], own[k])
            result_copy(k, 0, 4, me - 2).start()
            out[k, 0] = gram(own[k], far[k])

    @pl.loop(0, owned + 1)
    def _(k):
        @pl.when(k < owned)
        def _():
            pass_on(k)

        @pl.when(k >= 1)
        def _():
            correlate(k - 1)

    @pl.when(me < 2)
    def _():
        out[:, 0] = jnp.zeros_like(out[:, 0])

    @pl.when(me < 1)
    def _():
        out[:, 1] = jnp.zeros_like(out[:, 1])

    @pl.when(me + 1 >= blocks)
    def _():
        out[:, 3] = jnp.zeros_like(out[:, 3])

    @pl.when(me + 2 >= blocks)
    def _():
        out[:, 4] = jnp.zeros_like(out[:, 4])

    @pl.loop(0, owned)
    def _(k):
        @pl.when(even & has_down)
        def _():
            down_copy(k).wait_send()
            result_copy(k, 1, 0, me).wait_recv()
            result_copy(k, 2, 1, me).wait_recv()

        @pl.when(odd)
        def _():
            mate_copy(k).wait_send()
            result_copy(k, 0, 1, me).wait_recv()

        @pl.when(odd & has_up)
        def _():
            up_copy(k).wait_send()
            result_copy(k, 3, 3, me).wait_recv()
            result_copy(k, 0, 4, me).wait_recv()

        @pl.when(even)
        def _():
            result_copy(k, 0, 1, me + 1).wait_send()

        @pl.when(even & has_up)
        def _():
            result_copy(k, 1, 0, me + 2).wait_send()
            result_copy(k, 2, 1, me + 2).wait_send()
            result_copy(k, 3, 3, me + 1).wait_send()

        @pl.when(odd & has_down)
        def _():
            result_copy(k, 0, 4, me - 2).wait_send()


def correlate(grouped, sums):
    bins, per_bin, frames = grouped.shape
    blocks, modules = lax.axis_size("frame"), lax.axis_size("module")
    owned = bins // modules
    pixels = per_bin * modules
    vmem = pl.BlockSpec(memory_space=pltpu.VMEM)
    dma = pltpu.SemaphoreType.DMA
    return pl.pallas_call(
        functools.partial(correlate_kernel, blocks, modules),
        out_shape=jax.ShapeDtypeStruct((owned, 5, frames, frames), jnp.float32),
        in_specs=[vmem, vmem],
        out_specs=vmem,
        scratch_shapes=[
            pltpu.VMEM((modules, bins, frames), jnp.float32),
            pltpu.VMEM((bins, per_bin, frames), jnp.bfloat16),
            pltpu.VMEM((owned, pixels, frames), jnp.bfloat16),
            pltpu.VMEM((owned, pixels, frames), jnp.bfloat16),
            pltpu.VMEM((owned, pixels, frames), jnp.bfloat16),
            pltpu.VMEM((4, owned, frames, frames), jnp.float32),
            dma((modules - 1,)),
            dma((modules - 1,)),
            dma((owned, modules - 1)),
            dma((owned, modules - 1)),
            dma((2, owned)),
            dma((2, owned)),
            dma((4, owned)),
            dma((5, owned)),
        ],
        compiler_params=pltpu.CompilerParams(
            collective_id=0, has_side_effects=True, vmem_limit_bytes=VMEM_BYTES
        ),
    )(grouped, sums)


def per_device(raw_frames, dark_frame, flat_field, membership):
    bins, pixels = membership.shape
    labels = jnp.sum(membership * jnp.arange(bins, dtype=jnp.int32)[:, None], axis=0)
    place = jnp.arange(pixels, dtype=jnp.int32)
    keys = jnp.sort(labels * pixels + place)
    order = keys - place // (pixels // bins) * pixels
    grouped, sums = group_by_bin(order, raw_frames, dark_frame, flat_field, bins)
    return correlate(grouped, sums)[:, None]


def solution(mesh):
    in_specs = (P("frame", "module"), P("module"), P("module"), P(None, "module"))
    out_specs = P("module", "frame", None, None, None)
    return jax.shard_map(
        per_device, mesh=mesh, in_specs=in_specs, out_specs=out_specs, check_vma=False
    )
```

```python
import functools

import jax
import jax.numpy as jnp
from jax import lax
from jax.experimental import pallas as pl
from jax.experimental.pallas import tpu as pltpu
from jax.sharding import PartitionSpec as P

MESH = pl.DeviceIdType.MESH
VMEM_BYTES = 60 * 1024 * 1024


def group_kernel(per_bin, order, raw, dark, flat, grouped, sums, turned):
    step = pl.program_id(0)
    chunk = raw.shape[1]
    intensity = (raw[...].astype(jnp.float32) - dark[...]) * flat[...]
    turned[pl.ds(pl.multiple_of(step * chunk, chunk), chunk), :] = intensity.T

    @pl.when(step == pl.num_programs(0) - 1)
    def _():
        frames = turned.shape[1]
        lane = lax.broadcasted_iota(jnp.int32, (8, frames), 0)

        @pl.loop(0, grouped.shape[0])
        def _(label):
            base = label * per_bin

            def rows(group, total):
                first = pl.multiple_of(group * 8, 8)
                tile = jnp.broadcast_to(turned[pl.ds(order[base + first], 1), :], (8, frames))
                for row in range(1, 8):
                    line = turned[pl.ds(order[base + first + row], 1), :]
                    tile = jnp.where(lane == row, line, tile)
                grouped[label, pl.ds(first, 8), :] = tile
                return total + tile

            total = lax.fori_loop(0, per_bin // 8, rows, jnp.zeros((8, frames), jnp.float32), unroll=4)
            sums[pl.ds(label, 1), :] = jnp.sum(total, axis=0, keepdims=True)


def group_by_bin(order, raw_frames, dark_frame, flat_field, bins):
    frames, pixels = raw_frames.shape
    per_bin = pixels // bins
    chunk = per_bin
    return pl.pallas_call(
        functools.partial(group_kernel, per_bin),
        out_shape=(
            jax.ShapeDtypeStruct((bins, per_bin, frames), jnp.float32),
            jax.ShapeDtypeStruct((bins, frames), jnp.float32),
        ),
        grid_spec=pltpu.PrefetchScalarGridSpec(
            num_scalar_prefetch=1,
            grid=(pixels // chunk,),
            in_specs=[
                pl.BlockSpec((frames, chunk), lambda i, o: (0, i)),
                pl.BlockSpec((1, chunk), lambda i, o: (0, i)),
                pl.BlockSpec((1, chunk), lambda i, o: (0, i)),
            ],
            out_specs=(
                pl.BlockSpec((bins, per_bin, frames), lambda i, o: (0, 0, 0)),
                pl.BlockSpec((bins, frames), lambda i, o: (0, 0)),
            ),
            scratch_shapes=[pltpu.VMEM((pixels, frames), jnp.float32)],
        ),
        compiler_params=pltpu.CompilerParams(vmem_limit_bytes=VMEM_BYTES),
    )(order, raw_frames, dark_frame[None, :], flat_field[None, :])


def gram(left, right):
    return lax.dot_general(
        left, right, (((0,), (0,)), ((), ())), preferred_element_type=jnp.float32
    )


def correlate_kernel(
    blocks,
    modules,
    grouped,
    sums,
    out,
    all_sums,
    scaled,
    own,
    far,
    near,
    hold,
    staged,
    sum_send,
    sum_recv,
    bin_send,
    bin_recv,
    frame_send,
    frame_recv,
    relay_send,
    relay_recv,
    result_send,
    result_recv,
):
    me = lax.axis_index("frame")
    module = lax.axis_index("module")
    bins, per_bin, _ = grouped.shape
    owned = bins // modules
    even = lax.rem(me, 2) == 0
    odd = lax.rem(me, 2) == 1
    has_down = me >= 2
    has_up = me + 2 < blocks
    mate = me + 1 - 2 * lax.rem(me, 2)
    relayed = blocks == 8
    across = lax.rem(me + 4, 8)
    relaying = (me < 2) | (me >= 6)
    relay_parity = jnp.where(me >= 6, 1 - lax.rem(me, 2), lax.rem(me, 2))
    relay_target = jnp.where(even, 2, 5)

    barrier = pltpu.get_barrier_semaphore()

    def greet(frame, mod):
        pl.semaphore_signal(barrier, inc=1, device_id=(frame, mod), device_id_type=MESH)

    for gap in range(1, modules):
        greet(me, lax.rem(module + gap, modules))
    greet(mate, module)
    if relayed:
        greet(across, module)

    @pl.when(has_down)
    def _():
        greet(me - 2, module)

    @pl.when(has_up)
    def _():
        greet(me + 2, module)

    peers = modules + int(relayed) + has_down.astype(jnp.int32) + has_up.astype(jnp.int32)
    pl.semaphore_wait(barrier, peers)

    def sum_copy(gap):
        return pltpu.make_async_remote_copy(
            src_ref=sums,
            dst_ref=all_sums.at[module],
            send_sem=sum_send.at[gap - 1],
            recv_sem=sum_recv.at[gap - 1],
            device_id=(me, lax.rem(module + gap, modules)),
            device_id_type=MESH,
        )

    for gap in range(1, modules):
        sum_copy(gap).start()
    all_sums[module] = sums[...]
    for gap in range(1, modules):
        sum_copy(gap).wait()
    total = all_sums[0]
    for source in range(1, modules):
        total = total + all_sums[source]
    all_sums[0] = jnp.sqrt(jnp.float32(per_bin * modules)) / total

    def bin_copy(k, gap):
        owner = lax.rem(module + gap, modules)
        return pltpu.make_async_remote_copy(
            src_ref=scaled.at[owner * owned + k],
            dst_ref=own.at[k, pl.ds(pl.multiple_of(module * per_bin, per_bin), per_bin), :],
            send_sem=bin_send.at[k, gap - 1],
            recv_sem=bin_recv.at[k, gap - 1],
            device_id=(me, owner),
            device_id_type=MESH,
        )

    @pl.loop(0, owned)
    def _(k):
        for gap in range(1, modules):
            label = lax.rem(module + gap, modules) * owned + k
            factor = all_sums[0, pl.ds(label, 1), :]
            scaled[label] = (grouped[label] * factor).astype(jnp.bfloat16)
            bin_copy(k, gap).start()
        label = module * owned + k
        factor = all_sums[0, pl.ds(label, 1), :]
        own[k, pl.ds(pl.multiple_of(module * per_bin, per_bin), per_bin), :] = (
            grouped[label] * factor
        ).astype(jnp.bfloat16)

    def rows_of(j):
        source = lax.rem(module + modules - j, modules)
        return pl.ds(pl.multiple_of(source * per_bin, per_bin), per_bin)

    def frame_copy(k, j, slot, target, frame):
        return pltpu.make_async_remote_copy(
            src_ref=own.at[k, rows_of(j), :],
            dst_ref=target.at[k, rows_of(j), :],
            send_sem=frame_send.at[slot, k, j],
            recv_sem=frame_recv.at[slot, k, j],
            device_id=(frame, module),
            device_id_type=MESH,
        )

    def far_copy(k, j):
        return frame_copy(k, j, 0, far, jnp.where(even, me - 2, me + 2))

    def mate_copy(k, j):
        return frame_copy(k, j, 1, near, mate)

    def entry_copy(k, j):
        straight = jnp.where(even, me + 2, me - 2)
        return pltpu.make_async_remote_copy(
            src_ref=own.at[k, rows_of(j), :],
            dst_ref=hold.at[k, rows_of(j), :],
            send_sem=frame_send.at[0, k, j],
            recv_sem=relay_recv.at[k, j],
            device_id=(jnp.where(lax.rem(k, 2) == 0, across, straight), module),
            device_id_type=MESH,
        )

    def exit_copy(k, j):
        return pltpu.make_async_remote_copy(
            src_ref=hold.at[k, rows_of(j), :],
            dst_ref=far.at[k, rows_of(j), :],
            send_sem=relay_send.at[k, j],
            recv_sem=frame_recv.at[0, k, j],
            device_id=(relay_target, module),
            device_id_type=MESH,
        )

    sends_far = (even & has_down) | (odd & has_up)
    diagonal = ((me == 3) | (me == 4)) if relayed else None

    def result_copy(k, stage, place, frame):
        return pltpu.make_async_remote_copy(
            src_ref=staged.at[stage, k],
            dst_ref=out.at[k, place],
            send_sem=result_send.at[stage, k],
            recv_sem=result_recv.at[place, k],
            device_id=(frame, module),
            device_id_type=MESH,
        )

    def pass_on(k, j):
        @pl.when(odd)
        def _():
            mate_copy(k, j).start()

        if relayed:
            @pl.when(diagonal)
            def _():
                entry_copy(k, j).start()

            @pl.when(sends_far & jnp.logical_not(diagonal))
            def _():
                far_copy(k, j).start()
        else:
            @pl.when(sends_far)
            def _():
                far_copy(k, j).start()

    def relay(k, j):
        if relayed:
            @pl.when(relaying & (lax.rem(k, 2) == relay_parity))
            def _():
                entry_copy(k, j).wait_recv()
                exit_copy(k, j).start()

    def await_frames(k, copy):
        for j in range(modules):
            copy(k, j).wait_recv()

    def correlate(k):
        out[k, 2] = gram(own[k], own[k])

        @pl.when(even)
        def _():
            await_frames(k, mate_copy)
            staged[0, k] = gram(near[k], own[k])
            result_copy(k, 0, 1, me + 1).start()
            out[k, 3] = gram(own[k], near[k])

        @pl.when(even & has_up)
        def _():
            await_frames(k, far_copy)
            staged[1, k] = gram(far[k], own[k])
            result_copy(k, 1, 0, me + 2).start()
            staged[2, k] = gram(far[k], near[k])
            result_copy(k, 2, 1, me + 2).start()
            staged[3, k] = gram(near[k], far[k])
            result_copy(k, 3, 3, me + 1).start()
            out[k, 4] = gram(own[k], far[k])

        @pl.when(odd & has_down)
        def _():
            await_frames(k, far_copy)
            staged[0, k] = gram(far[k], own[k])
            result_copy(k, 0, 4, me - 2).start()
            out[k, 0] = gram(own[k], far[k])

    for k in range(owned):
        pass_on(k, 0)
    for k in range(owned):
        relay(k, 0)
    gaps = modules - 1

    @pl.loop(0, (owned + 1) * gaps)
    def _(step):
        k, j = step // gaps, lax.rem(step, gaps) + 1

        @pl.when(k < owned)
        def _():
            bin_copy(k, j).wait()
            pass_on(k, j)

        earlier = step - 1

        @pl.when((earlier >= 0) & (earlier < owned * gaps))
        def _():
            relay(earlier // gaps, lax.rem(earlier, gaps) + 1)

        @pl.when((k >= 1) & (j == gaps))
        def _():
            correlate(k - 1)

    @pl.when(me < 2)
    def _():
        out[:, 0] = jnp.zeros_like(out[:, 0])

    @pl.when(me < 1)
    def _():
        out[:, 1] = jnp.zeros_like(out[:, 1])

    @pl.when(me + 1 >= blocks)
    def _():
        out[:, 3] = jnp.zeros_like(out[:, 3])

    @pl.when(me + 2 >= blocks)
    def _():
        out[:, 4] = jnp.zeros_like(out[:, 4])

    @pl.loop(0, owned)
    def _(k):
        @pl.when(even & has_down)
        def _():
            result_copy(k, 1, 0, me).wait_recv()
            result_copy(k, 2, 1, me).wait_recv()

        @pl.when(odd)
        def _():
            for j in range(modules):
                mate_copy(k, j).wait_send()
            result_copy(k, 0, 1, me).wait_recv()

        @pl.when(sends_far)
        def _():
            for j in range(modules):
                far_copy(k, j).wait_send()

        @pl.when(odd & has_up)
        def _():
            result_copy(k, 3, 3, me).wait_recv()
            result_copy(k, 0, 4, me).wait_recv()

        if relayed:
            @pl.when(relaying & (lax.rem(k, 2) == relay_parity))
            def _():
                for j in range(modules):
                    exit_copy(k, j).wait_send()

        @pl.when(even)
        def _():
            result_copy(k, 0, 1, me + 1).wait_send()

        @pl.when(even & has_up)
        def _():
            result_copy(k, 1, 0, me + 2).wait_send()
            result_copy(k, 2, 1, me + 2).wait_send()
            result_copy(k, 3, 3, me + 1).wait_send()

        @pl.when(odd & has_down)
        def _():
            result_copy(k, 0, 4, me - 2).wait_send()


def correlate(grouped, sums):
    bins, per_bin, frames = grouped.shape
    blocks, modules = lax.axis_size("frame"), lax.axis_size("module")
    owned = bins // modules
    pixels = per_bin * modules
    vmem = pl.BlockSpec(memory_space=pltpu.VMEM)
    dma = pltpu.SemaphoreType.DMA
    return pl.pallas_call(
        functools.partial(correlate_kernel, blocks, modules),
        out_shape=jax.ShapeDtypeStruct((owned, 5, frames, frames), jnp.float32),
        in_specs=[vmem, vmem],
        out_specs=vmem,
        scratch_shapes=[
            pltpu.VMEM((modules, bins, frames), jnp.float32),
            pltpu.VMEM((bins, per_bin, frames), jnp.bfloat16),
            pltpu.VMEM((owned, pixels, frames), jnp.bfloat16),
            pltpu.VMEM((owned, pixels, frames), jnp.bfloat16),
            pltpu.VMEM((owned, pixels, frames), jnp.bfloat16),
            pltpu.VMEM((owned, pixels, frames), jnp.bfloat16),
            pltpu.VMEM((4, owned, frames, frames), jnp.float32),
            dma((modules - 1,)),
            dma((modules - 1,)),
            dma((owned, modules - 1)),
            dma((owned, modules - 1)),
            dma((2, owned, modules)),
            dma((2, owned, modules)),
            dma((owned, modules)),
            dma((owned, modules)),
            dma((4, owned)),
            dma((5, owned)),
        ],
        compiler_params=pltpu.CompilerParams(
            collective_id=0, has_side_effects=True, vmem_limit_bytes=VMEM_BYTES
        ),
    )(grouped, sums)


def per_device(raw_frames, dark_frame, flat_field, membership):
    bins, pixels = membership.shape
    labels = jnp.sum(membership * jnp.arange(bins, dtype=jnp.int32)[:, None], axis=0)
    place = jnp.arange(pixels, dtype=jnp.int32)
    keys = jnp.sort(labels * pixels + place)
    order = keys - place // (pixels // bins) * pixels
    grouped, sums = group_by_bin(order, raw_frames, dark_frame, flat_field, bins)
    return correlate(grouped, sums)[:, None]


def solution(mesh):
    in_specs = (P("frame", "module"), P("module"), P("module"), P(None, "module"))
    out_specs = P("module", "frame", None, None, None)
    return jax.shard_map(
        per_device, mesh=mesh, in_specs=in_specs, out_specs=out_specs, check_vma=False
    )
```

```python
import functools

import jax
import jax.numpy as jnp
from jax import lax
from jax.experimental import pallas as pl
from jax.experimental.pallas import tpu as pltpu
from jax.sharding import PartitionSpec as P

MESH = pl.DeviceIdType.MESH
VMEM_BYTES = 60 * 1024 * 1024


def turn_kernel(raw, dark, flat, members, turned, sums):
    @pl.when(pl.program_id(0) == 0)
    def _():
        sums[...] = jnp.zeros_like(sums)

    intensity = (raw[...].astype(jnp.float32) - dark[...]) * flat[...]
    lines = intensity.T
    turned[...] = lines
    sums[...] += jnp.dot(
        members[...].astype(jnp.float32),
        lines,
        precision=lax.Precision.HIGHEST,
        preferred_element_type=jnp.float32,
    )


def turn(raw_frames, dark_frame, flat_field, membership):
    frames, pixels = raw_frames.shape
    bins = membership.shape[0]
    chunk = pixels // bins
    return pl.pallas_call(
        turn_kernel,
        out_shape=(
            jax.ShapeDtypeStruct((pixels, frames), jnp.float32),
            jax.ShapeDtypeStruct((bins, frames), jnp.float32),
        ),
        grid=(pixels // chunk,),
        in_specs=[
            pl.BlockSpec((frames, chunk), lambda i: (0, i)),
            pl.BlockSpec((1, chunk), lambda i: (0, i)),
            pl.BlockSpec((1, chunk), lambda i: (0, i)),
            pl.BlockSpec((bins, chunk), lambda i: (0, i)),
        ],
        out_specs=(
            pl.BlockSpec((chunk, frames), lambda i: (i, 0)),
            pl.BlockSpec((bins, frames), lambda i: (0, 0)),
        ),
    )(raw_frames, dark_frame[None, :], flat_field[None, :], membership)


def gram(left, right):
    return lax.dot_general(
        left, right, (((0,), (0,)), ((), ())), preferred_element_type=jnp.float32
    )


def correlate_kernel(
    blocks,
    modules,
    order,
    turned,
    sums,
    out,
    all_sums,
    scaled,
    own,
    far,
    near,
    hold,
    staged,
    sum_send,
    sum_recv,
    bin_send,
    bin_recv,
    frame_send,
    frame_recv,
    relay_send,
    relay_recv,
    result_send,
    result_recv,
):
    me = lax.axis_index("frame")
    module = lax.axis_index("module")
    pixels, frames = turned.shape
    bins = sums.shape[0]
    per_bin = pixels // bins
    owned = bins // modules
    even = lax.rem(me, 2) == 0
    odd = lax.rem(me, 2) == 1
    has_down = me >= 2
    has_up = me + 2 < blocks
    mate = me + 1 - 2 * lax.rem(me, 2)
    relayed = blocks == 8
    across = lax.rem(me + 4, 8)
    relaying = (me < 2) | (me >= 6)
    relay_parity = jnp.where(me >= 6, 1 - lax.rem(me, 2), lax.rem(me, 2))
    relay_target = jnp.where(even, 2, 5)

    barrier = pltpu.get_barrier_semaphore()

    def greet(frame, mod):
        pl.semaphore_signal(barrier, inc=1, device_id=(frame, mod), device_id_type=MESH)

    for gap in range(1, modules):
        greet(me, lax.rem(module + gap, modules))
    greet(mate, module)
    if relayed:
        greet(across, module)

    @pl.when(has_down)
    def _():
        greet(me - 2, module)

    @pl.when(has_up)
    def _():
        greet(me + 2, module)

    peers = modules + int(relayed) + has_down.astype(jnp.int32) + has_up.astype(jnp.int32)
    pl.semaphore_wait(barrier, peers)

    def sum_copy(gap):
        return pltpu.make_async_remote_copy(
            src_ref=sums,
            dst_ref=all_sums.at[module],
            send_sem=sum_send.at[gap - 1],
            recv_sem=sum_recv.at[gap - 1],
            device_id=(me, lax.rem(module + gap, modules)),
            device_id_type=MESH,
        )

    for gap in range(1, modules):
        sum_copy(gap).start()
    all_sums[module] = sums[...]
    for gap in range(1, modules):
        sum_copy(gap).wait()
    total = all_sums[0]
    for source in range(1, modules):
        total = total + all_sums[source]
    all_sums[0] = jnp.sqrt(jnp.float32(per_bin * modules)) / total

    def bin_copy(k, gap):
        owner = lax.rem(module + gap, modules)
        return pltpu.make_async_remote_copy(
            src_ref=scaled.at[owner * owned + k],
            dst_ref=own.at[k, pl.ds(pl.multiple_of(module * per_bin, per_bin), per_bin), :],
            send_sem=bin_send.at[k, gap - 1],
            recv_sem=bin_recv.at[k, gap - 1],
            device_id=(me, owner),
            device_id_type=MESH,
        )

    row_index = lax.broadcasted_iota(jnp.int32, (8, frames), 0)

    def fill(label, target, first):
        factor = all_sums[0, pl.ds(label, 1), :]

        def tile(start):
            lines = jnp.broadcast_to(turned[pl.ds(order[start], 1), :], (8, frames))
            for row in range(1, 8):
                line = turned[pl.ds(order[start + row], 1), :]
                lines = jnp.where(row_index == row, line, lines)
            return lines * factor

        def tiles(group, carry):
            start = label * per_bin + group * 16
            both = jnp.concatenate([tile(start), tile(start + 8)], axis=0)
            rows = pl.ds(pl.multiple_of(first + group * 16, 16), 16)
            target[rows, :] = both.astype(jnp.bfloat16)
            return carry

        lax.fori_loop(0, per_bin // 16, tiles, 0, unroll=4)

    def rows_of(j):
        source = lax.rem(module + modules - j, modules)
        return pl.ds(pl.multiple_of(source * per_bin, per_bin), per_bin)

    def frame_copy(k, j, slot, target, frame):
        return pltpu.make_async_remote_copy(
            src_ref=own.at[k, rows_of(j), :],
            dst_ref=target.at[k, rows_of(j), :],
            send_sem=frame_send.at[slot, k, j],
            recv_sem=frame_recv.at[slot, k, j],
            device_id=(frame, module),
            device_id_type=MESH,
        )

    def far_copy(k, j):
        return frame_copy(k, j, 0, far, jnp.where(even, me - 2, me + 2))

    def mate_copy(k, j):
        return frame_copy(k, j, 1, near, mate)

    def entry_copy(k, j):
        straight = jnp.where(even, me + 2, me - 2)
        return pltpu.make_async_remote_copy(
            src_ref=own.at[k, rows_of(j), :],
            dst_ref=hold.at[k, rows_of(j), :],
            send_sem=frame_send.at[0, k, j],
            recv_sem=relay_recv.at[k, j],
            device_id=(jnp.where(lax.rem(k, 2) == 0, across, straight), module),
            device_id_type=MESH,
        )

    def exit_copy(k, j):
        return pltpu.make_async_remote_copy(
            src_ref=hold.at[k, rows_of(j), :],
            dst_ref=far.at[k, rows_of(j), :],
            send_sem=relay_send.at[k, j],
            recv_sem=frame_recv.at[0, k, j],
            device_id=(relay_target, module),
            device_id_type=MESH,
        )

    sends_far = (even & has_down) | (odd & has_up)
    diagonal = ((me == 3) | (me == 4)) if relayed else None

    def result_copy(k, stage, place, frame):
        return pltpu.make_async_remote_copy(
            src_ref=staged.at[stage, k],
            dst_ref=out.at[k, place],
            send_sem=result_send.at[stage, k],
            recv_sem=result_recv.at[place, k],
            device_id=(frame, module),
            device_id_type=MESH,
        )

    def pass_on(k, j):
        @pl.when(odd)
        def _():
            mate_copy(k, j).start()

        if relayed:
            @pl.when(diagonal)
            def _():
                entry_copy(k, j).start()

            @pl.when(sends_far & jnp.logical_not(diagonal))
            def _():
                far_copy(k, j).start()
        else:
            @pl.when(sends_far)
            def _():
                far_copy(k, j).start()

    def relay(k, j):
        if relayed:
            @pl.when(relaying & (lax.rem(k, 2) == relay_parity))
            def _():
                entry_copy(k, j).wait_recv()
                exit_copy(k, j).start()

    def await_frames(k, copy):
        for j in range(modules):
            copy(k, j).wait_recv()

    def correlate(k):
        out[k, 2] = gram(own[k], own[k])

        @pl.when(even)
        def _():
            await_frames(k, mate_copy)
            staged[0, k] = gram(near[k], own[k])
            result_copy(k, 0, 1, me + 1).start()
            out[k, 3] = gram(own[k], near[k])

        @pl.when(even & has_up)
        def _():
            await_frames(k, far_copy)
            staged[1, k] = gram(far[k], own[k])
            result_copy(k, 1, 0, me + 2).start()
            staged[2, k] = gram(far[k], near[k])
            result_copy(k, 2, 1, me + 2).start()
            staged[3, k] = gram(near[k], far[k])
            result_copy(k, 3, 3, me + 1).start()
            out[k, 4] = gram(own[k], far[k])

        @pl.when(odd & has_down)
        def _():
            await_frames(k, far_copy)
            staged[0, k] = gram(far[k], own[k])
            result_copy(k, 0, 4, me - 2).start()
            out[k, 0] = gram(own[k], far[k])

    @pl.loop(0, owned)
    def _(k):
        @pl.loop(1, modules)
        def _(gap):
            label = lax.rem(module + gap, modules) * owned + k
            fill(label, scaled.at[label], 0)
            bin_copy(k, gap).start()

        fill(module * owned + k, own.at[k], module * per_bin)
        pass_on(k, 0)

    for k in range(owned):
        relay(k, 0)
    gaps = modules - 1

    @pl.loop(0, (owned + 1) * gaps)
    def _(step):
        k, j = step // gaps, lax.rem(step, gaps) + 1

        @pl.when(k < owned)
        def _():
            bin_copy(k, j).wait()
            pass_on(k, j)

        earlier = step - 1

        @pl.when((earlier >= 0) & (earlier < owned * gaps))
        def _():
            relay(earlier // gaps, lax.rem(earlier, gaps) + 1)

        @pl.when((k >= 1) & (j == gaps))
        def _():
            correlate(k - 1)

    @pl.when(me < 2)
    def _():
        out[:, 0] = jnp.zeros_like(out[:, 0])

    @pl.when(me < 1)
    def _():
        out[:, 1] = jnp.zeros_like(out[:, 1])

    @pl.when(me + 1 >= blocks)
    def _():
        out[:, 3] = jnp.zeros_like(out[:, 3])

    @pl.when(me + 2 >= blocks)
    def _():
        out[:, 4] = jnp.zeros_like(out[:, 4])

    @pl.loop(0, owned)
    def _(k):
        @pl.when(even & has_down)
        def _():
            result_copy(k, 1, 0, me).wait_recv()
            result_copy(k, 2, 1, me).wait_recv()

        @pl.when(odd)
        def _():
            for j in range(modules):
                mate_copy(k, j).wait_send()
            result_copy(k, 0, 1, me).wait_recv()

        @pl.when(sends_far)
        def _():
            for j in range(modules):
                far_copy(k, j).wait_send()

        @pl.when(odd & has_up)
        def _():
            result_copy(k, 3, 3, me).wait_recv()
            result_copy(k, 0, 4, me).wait_recv()

        if relayed:
            @pl.when(relaying & (lax.rem(k, 2) == relay_parity))
            def _():
                for j in range(modules):
                    exit_copy(k, j).wait_send()

        @pl.when(even)
        def _():
            result_copy(k, 0, 1, me + 1).wait_send()

        @pl.when(even & has_up)
        def _():
            result_copy(k, 1, 0, me + 2).wait_send()
            result_copy(k, 2, 1, me + 2).wait_send()
            result_copy(k, 3, 3, me + 1).wait_send()

        @pl.when(odd & has_down)
        def _():
            result_copy(k, 0, 4, me - 2).wait_send()


def correlate(order, turned, sums):
    (pixels, frames), bins = turned.shape, sums.shape[0]
    per_bin = pixels // bins
    blocks, modules = lax.axis_size("frame"), lax.axis_size("module")
    owned = bins // modules
    gathered = per_bin * modules
    vmem = pl.BlockSpec(memory_space=pltpu.VMEM)
    dma = pltpu.SemaphoreType.DMA
    return pl.pallas_call(
        functools.partial(correlate_kernel, blocks, modules),
        out_shape=jax.ShapeDtypeStruct((owned, 5, frames, frames), jnp.float32),
        in_specs=[pl.BlockSpec(memory_space=pltpu.SMEM), vmem, vmem],
        out_specs=vmem,
        scratch_shapes=[
            pltpu.VMEM((modules, bins, frames), jnp.float32),
            pltpu.VMEM((bins, per_bin, frames), jnp.bfloat16),
            pltpu.VMEM((owned, gathered, frames), jnp.bfloat16),
            pltpu.VMEM((owned, gathered, frames), jnp.bfloat16),
            pltpu.VMEM((owned, gathered, frames), jnp.bfloat16),
            pltpu.VMEM((owned, gathered, frames), jnp.bfloat16),
            pltpu.VMEM((4, owned, frames, frames), jnp.float32),
            dma((modules - 1,)),
            dma((modules - 1,)),
            dma((owned, modules - 1)),
            dma((owned, modules - 1)),
            dma((2, owned, modules)),
            dma((2, owned, modules)),
            dma((owned, modules)),
            dma((owned, modules)),
            dma((4, owned)),
            dma((5, owned)),
        ],
        compiler_params=pltpu.CompilerParams(
            collective_id=0, has_side_effects=True, vmem_limit_bytes=VMEM_BYTES
        ),
    )(order, turned, sums)


def per_device(raw_frames, dark_frame, flat_field, membership):
    bins, pixels = membership.shape
    labels = jnp.sum(membership * jnp.arange(bins, dtype=jnp.int32)[:, None], axis=0)
    place = jnp.arange(pixels, dtype=jnp.int32)
    keys = jnp.sort(labels * pixels + place)
    order = keys - place // (pixels // bins) * pixels
    turned, sums = turn(raw_frames, dark_frame, flat_field, membership)
    return correlate(order, turned, sums)[:, None]


def solution(mesh):
    in_specs = (P("frame", "module"), P("module"), P("module"), P(None, "module"))
    out_specs = P("module", "frame", None, None, None)
    return jax.shard_map(
        per_device, mesh=mesh, in_specs=in_specs, out_specs=out_specs, check_vma=False
    )
```

```python
import functools

import jax
import jax.numpy as jnp
from jax import lax
from jax.experimental import pallas as pl
from jax.experimental.pallas import tpu as pltpu
from jax.sharding import PartitionSpec as P

MESH = pl.DeviceIdType.MESH
VMEM_BYTES = 60 * 1024 * 1024


def turn_kernel(raw, dark, flat, members, turned, sums):
    @pl.when(pl.program_id(0) == 0)
    def _():
        sums[...] = jnp.zeros_like(sums)

    intensity = (raw[...].astype(jnp.float32) - dark[...]) * flat[...]
    lines = intensity.T
    turned[...] = lines
    sums[...] += jnp.dot(
        members[...].astype(jnp.float32),
        lines,
        precision=lax.Precision.HIGHEST,
        preferred_element_type=jnp.float32,
    )


def turn(raw_frames, dark_frame, flat_field, membership):
    frames, pixels = raw_frames.shape
    bins = membership.shape[0]
    chunk = pixels // bins
    return pl.pallas_call(
        turn_kernel,
        out_shape=(
            jax.ShapeDtypeStruct((pixels, frames), jnp.float32),
            jax.ShapeDtypeStruct((bins, frames), jnp.float32),
        ),
        grid=(pixels // chunk,),
        in_specs=[
            pl.BlockSpec((frames, chunk), lambda i: (0, i)),
            pl.BlockSpec((1, chunk), lambda i: (0, i)),
            pl.BlockSpec((1, chunk), lambda i: (0, i)),
            pl.BlockSpec((bins, chunk), lambda i: (0, i)),
        ],
        out_specs=(
            pl.BlockSpec((chunk, frames), lambda i: (i, 0)),
            pl.BlockSpec((bins, frames), lambda i: (0, 0)),
        ),
    )(raw_frames, dark_frame[None, :], flat_field[None, :], membership)


def gram(left, right):
    return lax.dot_general(
        left, right, (((0,), (0,)), ((), ())), preferred_element_type=jnp.float32
    )


def correlate_kernel(
    blocks,
    modules,
    order,
    turned,
    sums,
    out,
    all_sums,
    scaled,
    own,
    far,
    near,
    hold,
    staged,
    sum_send,
    sum_recv,
    bin_send,
    bin_recv,
    frame_send,
    frame_recv,
    relay_send,
    relay_recv,
    result_send,
    result_recv,
):
    me = lax.axis_index("frame")
    module = lax.axis_index("module")
    pixels, frames = turned.shape
    bins = sums.shape[0]
    per_bin = pixels // bins
    owned = bins // modules
    even = lax.rem(me, 2) == 0
    odd = lax.rem(me, 2) == 1
    has_down = me >= 2
    has_up = me + 2 < blocks
    mate = me + 1 - 2 * lax.rem(me, 2)
    relayed = blocks == 8
    across = lax.rem(me + 4, 8)
    relaying = (me < 2) | (me >= 6)
    relay_parity = jnp.where(me >= 6, 1 - lax.rem(me, 2), lax.rem(me, 2))
    relay_target = jnp.where(even, 2, 5)

    barrier = pltpu.get_barrier_semaphore()

    def greet(frame, mod):
        pl.semaphore_signal(barrier, inc=1, device_id=(frame, mod), device_id_type=MESH)

    for gap in range(1, modules):
        greet(me, lax.rem(module + gap, modules))
    greet(mate, module)
    if relayed:
        greet(across, module)

    @pl.when(has_down)
    def _():
        greet(me - 2, module)

    @pl.when(has_up)
    def _():
        greet(me + 2, module)

    peers = modules + int(relayed) + has_down.astype(jnp.int32) + has_up.astype(jnp.int32)
    pl.semaphore_wait(barrier, peers)

    def sum_copy(gap):
        return pltpu.make_async_remote_copy(
            src_ref=sums,
            dst_ref=all_sums.at[module],
            send_sem=sum_send.at[gap - 1],
            recv_sem=sum_recv.at[gap - 1],
            device_id=(me, lax.rem(module + gap, modules)),
            device_id_type=MESH,
        )

    for gap in range(1, modules):
        sum_copy(gap).start()
    all_sums[module] = sums[...]
    for gap in range(1, modules):
        sum_copy(gap).wait()
    total = all_sums[0]
    for source in range(1, modules):
        total = total + all_sums[source]
    all_sums[0] = jnp.sqrt(jnp.float32(per_bin * modules)) / total

    half = per_bin // 2
    parts = 2 * modules

    def bin_copy(k, piece):
        gap, part = piece // 2, lax.rem(piece, 2)
        owner = lax.rem(module + gap, modules)
        start = pl.multiple_of(part * half, half)
        landing = pl.multiple_of(module * per_bin + part * half, half)
        return pltpu.make_async_remote_copy(
            src_ref=scaled.at[owner * owned + k, pl.ds(start, half), :],
            dst_ref=own.at[k, pl.ds(landing, half), :],
            send_sem=bin_send.at[k, piece],
            recv_sem=bin_recv.at[k, piece],
            device_id=(me, owner),
            device_id_type=MESH,
        )

    row_index = lax.broadcasted_iota(jnp.int32, (8, frames), 0)

    def fill(label, target, first):
        factor = all_sums[0, pl.ds(label, 1), :]

        def tile(start):
            lines = jnp.broadcast_to(turned[pl.ds(order[start], 1), :], (8, frames))
            for row in range(1, 8):
                line = turned[pl.ds(order[start + row], 1), :]
                lines = jnp.where(row_index == row, line, lines)
            return lines * factor

        def tiles(group, carry):
            start = label * per_bin + group * 16
            both = jnp.concatenate([tile(start), tile(start + 8)], axis=0)
            rows = pl.ds(pl.multiple_of(first + group * 16, 16), 16)
            target[rows, :] = both.astype(jnp.bfloat16)
            return carry

        lax.fori_loop(0, per_bin // 16, tiles, 0, unroll=4)

    def rows_of(j):
        source = lax.rem(module + modules - j // 2, modules)
        return pl.ds(pl.multiple_of(source * per_bin + lax.rem(j, 2) * half, half), half)

    def frame_copy(k, j, slot, target, frame):
        return pltpu.make_async_remote_copy(
            src_ref=own.at[k, rows_of(j), :],
            dst_ref=target.at[k, rows_of(j), :],
            send_sem=frame_send.at[slot, k, j],
            recv_sem=frame_recv.at[slot, k, j],
            device_id=(frame, module),
            device_id_type=MESH,
        )

    def far_copy(k, j):
        return frame_copy(k, j, 0, far, jnp.where(even, me - 2, me + 2))

    def mate_copy(k, j):
        return frame_copy(k, j, 1, near, mate)

    def entry_copy(k, j):
        straight = jnp.where(even, me + 2, me - 2)
        return pltpu.make_async_remote_copy(
            src_ref=own.at[k, rows_of(j), :],
            dst_ref=hold.at[k, rows_of(j), :],
            send_sem=frame_send.at[0, k, j],
            recv_sem=relay_recv.at[k, j],
            device_id=(jnp.where(lax.rem(k, 2) == 0, across, straight), module),
            device_id_type=MESH,
        )

    def exit_copy(k, j):
        return pltpu.make_async_remote_copy(
            src_ref=hold.at[k, rows_of(j), :],
            dst_ref=far.at[k, rows_of(j), :],
            send_sem=relay_send.at[k, j],
            recv_sem=frame_recv.at[0, k, j],
            device_id=(relay_target, module),
            device_id_type=MESH,
        )

    sends_far = (even & has_down) | (odd & has_up)
    diagonal = ((me == 3) | (me == 4)) if relayed else None

    def result_copy(k, stage, place, frame):
        return pltpu.make_async_remote_copy(
            src_ref=staged.at[stage, k],
            dst_ref=out.at[k, place],
            send_sem=result_send.at[stage, k],
            recv_sem=result_recv.at[place, k],
            device_id=(frame, module),
            device_id_type=MESH,
        )

    def pass_on(k, j):
        @pl.when(odd)
        def _():
            mate_copy(k, j).start()

        if relayed:
            @pl.when(diagonal)
            def _():
                entry_copy(k, j).start()

            @pl.when(sends_far & jnp.logical_not(diagonal))
            def _():
                far_copy(k, j).start()
        else:
            @pl.when(sends_far)
            def _():
                far_copy(k, j).start()

    def relay(k, j):
        if relayed:
            @pl.when(relaying & (lax.rem(k, 2) == relay_parity))
            def _():
                entry_copy(k, j).wait_recv()
                exit_copy(k, j).start()

    def await_frames(k, copy):
        for j in range(parts):
            copy(k, j).wait_recv()

    def correlate(k):
        out[k, 2] = gram(own[k], own[k])

        @pl.when(even)
        def _():
            await_frames(k, mate_copy)
            staged[0, k] = gram(near[k], own[k])
            result_copy(k, 0, 1, me + 1).start()
            out[k, 3] = gram(own[k], near[k])

        @pl.when(even & has_up)
        def _():
            await_frames(k, far_copy)
            staged[1, k] = gram(far[k], own[k])
            result_copy(k, 1, 0, me + 2).start()
            staged[2, k] = gram(far[k], near[k])
            result_copy(k, 2, 1, me + 2).start()
            staged[3, k] = gram(near[k], far[k])
            result_copy(k, 3, 3, me + 1).start()
            out[k, 4] = gram(own[k], far[k])

        @pl.when(odd & has_down)
        def _():
            await_frames(k, far_copy)
            staged[0, k] = gram(far[k], own[k])
            result_copy(k, 0, 4, me - 2).start()
            out[k, 0] = gram(own[k], far[k])

    @pl.loop(0, owned)
    def _(k):
        @pl.loop(1, modules)
        def _(gap):
            label = lax.rem(module + gap, modules) * owned + k
            fill(label, scaled.at[label], 0)
            bin_copy(k, 2 * gap).start()
            bin_copy(k, 2 * gap + 1).start()

        fill(module * owned + k, own.at[k], module * per_bin)
        pass_on(k, 0)
        pass_on(k, 1)

    @pl.loop(0, owned)
    def _(k):
        relay(k, 0)
        relay(k, 1)

    light = jnp.where(lax.rem(module, 2) == 1, 1, modules - 1)
    heavy = [lax.rem(light + i - 1, modules - 1) + 1 for i in range(1, modules - 1)]

    def receive(k, gaps):
        pieces = [2 * gap + part for part in range(2) for gap in gaps]
        for index, piece in enumerate(pieces):
            bin_copy(k, piece).wait()
            pass_on(k, piece)
            if index:
                relay(k, pieces[index - 1])
        relay(k, pieces[-1])

    @pl.loop(0, owned + 2)
    def _(turn_index):
        @pl.when(turn_index < owned)
        def _():
            receive(turn_index, [light])

        @pl.when((turn_index >= 1) & (turn_index <= owned))
        def _():
            receive(turn_index - 1, heavy)

        @pl.when(turn_index >= 2)
        def _():
            correlate(turn_index - 2)

    @pl.when(me < 2)
    def _():
        out[:, 0] = jnp.zeros_like(out[:, 0])

    @pl.when(me < 1)
    def _():
        out[:, 1] = jnp.zeros_like(out[:, 1])

    @pl.when(me + 1 >= blocks)
    def _():
        out[:, 3] = jnp.zeros_like(out[:, 3])

    @pl.when(me + 2 >= blocks)
    def _():
        out[:, 4] = jnp.zeros_like(out[:, 4])

    @pl.loop(0, owned)
    def _(k):
        @pl.when(even & has_down)
        def _():
            result_copy(k, 1, 0, me).wait_recv()
            result_copy(k, 2, 1, me).wait_recv()

        @pl.when(odd)
        def _():
            for j in range(parts):
                mate_copy(k, j).wait_send()
            result_copy(k, 0, 1, me).wait_recv()

        @pl.when(sends_far)
        def _():
            for j in range(parts):
                far_copy(k, j).wait_send()

        @pl.when(odd & has_up)
        def _():
            result_copy(k, 3, 3, me).wait_recv()
            result_copy(k, 0, 4, me).wait_recv()

        if relayed:
            @pl.when(relaying & (lax.rem(k, 2) == relay_parity))
            def _():
                for j in range(parts):
                    exit_copy(k, j).wait_send()

        @pl.when(even)
        def _():
            result_copy(k, 0, 1, me + 1).wait_send()

        @pl.when(even & has_up)
        def _():
            result_copy(k, 1, 0, me + 2).wait_send()
            result_copy(k, 2, 1, me + 2).wait_send()
            result_copy(k, 3, 3, me + 1).wait_send()

        @pl.when(odd & has_down)
        def _():
            result_copy(k, 0, 4, me - 2).wait_send()


def correlate(order, turned, sums):
    (pixels, frames), bins = turned.shape, sums.shape[0]
    per_bin = pixels // bins
    blocks, modules = lax.axis_size("frame"), lax.axis_size("module")
    owned = bins // modules
    gathered = per_bin * modules
    vmem = pl.BlockSpec(memory_space=pltpu.VMEM)
    dma = pltpu.SemaphoreType.DMA
    return pl.pallas_call(
        functools.partial(correlate_kernel, blocks, modules),
        out_shape=jax.ShapeDtypeStruct((owned, 5, frames, frames), jnp.float32),
        in_specs=[pl.BlockSpec(memory_space=pltpu.SMEM), vmem, vmem],
        out_specs=vmem,
        scratch_shapes=[
            pltpu.VMEM((modules, bins, frames), jnp.float32),
            pltpu.VMEM((bins, per_bin, frames), jnp.bfloat16),
            pltpu.VMEM((owned, gathered, frames), jnp.bfloat16),
            pltpu.VMEM((owned, gathered, frames), jnp.bfloat16),
            pltpu.VMEM((owned, gathered, frames), jnp.bfloat16),
            pltpu.VMEM((owned, gathered, frames), jnp.bfloat16),
            pltpu.VMEM((4, owned, frames, frames), jnp.float32),
            dma((modules - 1,)),
            dma((modules - 1,)),
            dma((owned, 2 * modules)),
            dma((owned, 2 * modules)),
            dma((2, owned, 2 * modules)),
            dma((2, owned, 2 * modules)),
            dma((owned, 2 * modules)),
            dma((owned, 2 * modules)),
            dma((4, owned)),
            dma((5, owned)),
        ],
        compiler_params=pltpu.CompilerParams(
            collective_id=0, has_side_effects=True, vmem_limit_bytes=VMEM_BYTES
        ),
    )(order, turned, sums)


def per_device(raw_frames, dark_frame, flat_field, membership):
    bins, pixels = membership.shape
    labels = jnp.sum(membership * jnp.arange(bins, dtype=jnp.int32)[:, None], axis=0)
    place = jnp.arange(pixels, dtype=jnp.int32)
    keys = jnp.sort(labels * pixels + place)
    order = keys - place // (pixels // bins) * pixels
    turned, sums = turn(raw_frames, dark_frame, flat_field, membership)
    return correlate(order, turned, sums)[:, None]


def solution(mesh):
    in_specs = (P("frame", "module"), P("module"), P("module"), P(None, "module"))
    out_specs = P("module", "frame", None, None, None)
    return jax.shard_map(
        per_device, mesh=mesh, in_specs=in_specs, out_specs=out_specs, check_vma=False
    )
```

```python
import functools

import jax
import jax.numpy as jnp
from jax import lax
from jax.experimental import pallas as pl
from jax.experimental.pallas import tpu as pltpu
from jax.sharding import PartitionSpec as P

MESH = pl.DeviceIdType.MESH
VMEM_BYTES = 60 * 1024 * 1024


def turn_kernel(raw, dark, flat, members, turned, sums):
    @pl.when(pl.program_id(0) == 0)
    def _():
        sums[...] = jnp.zeros_like(sums)

    intensity = (raw[...].astype(jnp.float32) - dark[...]) * flat[...]
    lines = intensity.T
    turned[...] = lines
    sums[...] += jnp.dot(
        members[...].astype(jnp.float32),
        lines,
        precision=lax.Precision.HIGHEST,
        preferred_element_type=jnp.float32,
    )


def turn(raw_frames, dark_frame, flat_field, membership):
    frames, pixels = raw_frames.shape
    bins = membership.shape[0]
    chunk = pixels // bins
    return pl.pallas_call(
        turn_kernel,
        out_shape=(
            jax.ShapeDtypeStruct((pixels, frames), jnp.float32),
            jax.ShapeDtypeStruct((bins, frames), jnp.float32),
        ),
        grid=(pixels // chunk,),
        in_specs=[
            pl.BlockSpec((frames, chunk), lambda i: (0, i)),
            pl.BlockSpec((1, chunk), lambda i: (0, i)),
            pl.BlockSpec((1, chunk), lambda i: (0, i)),
            pl.BlockSpec((bins, chunk), lambda i: (0, i)),
        ],
        out_specs=(
            pl.BlockSpec((chunk, frames), lambda i: (i, 0)),
            pl.BlockSpec((bins, frames), lambda i: (0, 0)),
        ),
    )(raw_frames, dark_frame[None, :], flat_field[None, :], membership)


def gram(left, right):
    return lax.dot_general(
        left, right, (((0,), (0,)), ((), ())), preferred_element_type=jnp.float32
    )


def correlate_kernel(
    blocks,
    modules,
    order,
    turned,
    sums,
    out,
    all_sums,
    scaled,
    own,
    far,
    near,
    hold,
    staged,
    sum_send,
    sum_recv,
    bin_send,
    bin_recv,
    frame_send,
    frame_recv,
    relay_send,
    relay_recv,
    result_send,
    result_recv,
):
    me = lax.axis_index("frame")
    module = lax.axis_index("module")
    pixels, frames = turned.shape
    bins = sums.shape[0]
    per_bin = pixels // bins
    owned = bins // modules
    even = lax.rem(me, 2) == 0
    odd = lax.rem(me, 2) == 1
    has_down = me >= 2
    has_up = me + 2 < blocks
    mate = me + 1 - 2 * lax.rem(me, 2)
    relayed = blocks == 8
    across = lax.rem(me + 4, 8)
    relaying = (me < 2) | (me >= 6)
    relay_parity = jnp.where(me >= 6, 1 - lax.rem(me, 2), lax.rem(me, 2))
    relay_target = jnp.where(even, 2, 5)

    barrier = pltpu.get_barrier_semaphore()

    def greet(frame, mod):
        pl.semaphore_signal(barrier, inc=1, device_id=(frame, mod), device_id_type=MESH)

    for gap in range(1, modules):
        greet(me, lax.rem(module + gap, modules))
    greet(mate, module)
    if relayed:
        greet(across, module)

    @pl.when(has_down)
    def _():
        greet(me - 2, module)

    @pl.when(has_up)
    def _():
        greet(me + 2, module)

    peers = modules + int(relayed) + has_down.astype(jnp.int32) + has_up.astype(jnp.int32)
    pl.semaphore_wait(barrier, peers)

    def sum_copy(gap):
        return pltpu.make_async_remote_copy(
            src_ref=sums,
            dst_ref=all_sums.at[module],
            send_sem=sum_send.at[gap - 1],
            recv_sem=sum_recv.at[gap - 1],
            device_id=(me, lax.rem(module + gap, modules)),
            device_id_type=MESH,
        )

    for gap in range(1, modules):
        sum_copy(gap).start()
    all_sums[module] = sums[...]
    for gap in range(1, modules):
        sum_copy(gap).wait()
    total = all_sums[0]
    for source in range(1, modules):
        total = total + all_sums[source]
    all_sums[0] = jnp.sqrt(jnp.float32(per_bin * modules)) / total

    half = per_bin // 2
    parts = 2 * modules

    def bin_copy(k, piece):
        gap, part = piece // 2, lax.rem(piece, 2)
        owner = lax.rem(module + gap, modules)
        start = pl.multiple_of(part * half, half)
        landing = pl.multiple_of(module * per_bin + part * half, half)
        return pltpu.make_async_remote_copy(
            src_ref=scaled.at[owner * owned + k, pl.ds(start, half), :],
            dst_ref=own.at[k, pl.ds(landing, half), :],
            send_sem=bin_send.at[k, piece],
            recv_sem=bin_recv.at[k, piece],
            device_id=(me, owner),
            device_id_type=MESH,
        )

    row_index = lax.broadcasted_iota(jnp.int32, (8, frames), 0)

    def fill(label, target, first):
        factor = all_sums[0, pl.ds(label, 1), :]

        def tile(start):
            lines = jnp.broadcast_to(turned[pl.ds(order[start], 1), :], (8, frames))
            for row in range(1, 8):
                line = turned[pl.ds(order[start + row], 1), :]
                lines = jnp.where(row_index == row, line, lines)
            return lines * factor

        def tiles(group, carry):
            start = label * per_bin + group * 16
            both = jnp.concatenate([tile(start), tile(start + 8)], axis=0)
            rows = pl.ds(pl.multiple_of(first + group * 16, 16), 16)
            target[rows, :] = both.astype(jnp.bfloat16)
            return carry

        lax.fori_loop(0, per_bin // 16, tiles, 0, unroll=4)

    def rows_of(j):
        source = lax.rem(module + modules - j // 2, modules)
        return pl.ds(pl.multiple_of(source * per_bin + lax.rem(j, 2) * half, half), half)

    def frame_copy(k, j, slot, target, frame):
        return pltpu.make_async_remote_copy(
            src_ref=own.at[k, rows_of(j), :],
            dst_ref=target.at[k, rows_of(j), :],
            send_sem=frame_send.at[slot, k, j],
            recv_sem=frame_recv.at[slot, k, j],
            device_id=(frame, module),
            device_id_type=MESH,
        )

    def far_copy(k, j):
        return frame_copy(k, j, 0, far, jnp.where(even, me - 2, me + 2))

    def mate_copy(k, j):
        return frame_copy(k, j, 1, near, mate)

    def entry_copy(k, j):
        straight = jnp.where(even, me + 2, me - 2)
        return pltpu.make_async_remote_copy(
            src_ref=own.at[k, rows_of(j), :],
            dst_ref=hold.at[k, rows_of(j), :],
            send_sem=frame_send.at[0, k, j],
            recv_sem=relay_recv.at[k, j],
            device_id=(jnp.where(lax.rem(k, 2) == 0, across, straight), module),
            device_id_type=MESH,
        )

    def exit_copy(k, j):
        return pltpu.make_async_remote_copy(
            src_ref=hold.at[k, rows_of(j), :],
            dst_ref=far.at[k, rows_of(j), :],
            send_sem=relay_send.at[k, j],
            recv_sem=frame_recv.at[0, k, j],
            device_id=(relay_target, module),
            device_id_type=MESH,
        )

    sends_far = (even & has_down) | (odd & has_up)
    diagonal = ((me == 3) | (me == 4)) if relayed else None

    def result_copy(k, stage, place, frame):
        return pltpu.make_async_remote_copy(
            src_ref=staged.at[stage, k],
            dst_ref=out.at[k, place],
            send_sem=result_send.at[stage, k],
            recv_sem=result_recv.at[place, k],
            device_id=(frame, module),
            device_id_type=MESH,
        )

    def pass_on(k, j):
        @pl.when(odd)
        def _():
            mate_copy(k, j).start()

        if relayed:
            @pl.when(diagonal)
            def _():
                entry_copy(k, j).start()

            @pl.when(sends_far & jnp.logical_not(diagonal))
            def _():
                far_copy(k, j).start()
        else:
            @pl.when(sends_far)
            def _():
                far_copy(k, j).start()

    def relay(k, j):
        if relayed:
            @pl.when(relaying & (lax.rem(k, 2) == relay_parity))
            def _():
                entry_copy(k, j).wait_recv()
                exit_copy(k, j).start()

    def await_frames(k, copy):
        for j in range(parts):
            copy(k, j).wait_recv()

    def correlate(k):
        out[k, 2] = gram(own[k], own[k])

        @pl.when(even)
        def _():
            await_frames(k, mate_copy)
            staged[0, k] = gram(near[k], own[k])
            result_copy(k, 0, 1, me + 1).start()
            out[k, 3] = gram(own[k], near[k])

        @pl.when(even & has_up)
        def _():
            await_frames(k, far_copy)
            staged[1, k] = gram(far[k], own[k])
            result_copy(k, 1, 0, me + 2).start()
            staged[2, k] = gram(far[k], near[k])
            result_copy(k, 2, 1, me + 2).start()
            staged[3, k] = gram(near[k], far[k])
            result_copy(k, 3, 3, me + 1).start()
            out[k, 4] = gram(own[k], far[k])

        @pl.when(odd & has_down)
        def _():
            await_frames(k, far_copy)
            staged[0, k] = gram(far[k], own[k])
            result_copy(k, 0, 4, me - 2).start()
            out[k, 0] = gram(own[k], far[k])

    @pl.loop(0, owned)
    def _(k):
        @pl.loop(1, modules)
        def _(gap):
            label = lax.rem(module + gap, modules) * owned + k
            fill(label, scaled.at[label], 0)
            bin_copy(k, 2 * gap).start()
            bin_copy(k, 2 * gap + 1).start()

        fill(module * owned + k, own.at[k], module * per_bin)
        pass_on(k, 0)
        pass_on(k, 1)

    @pl.loop(0, owned)
    def _(k):
        relay(k, 0)
        relay(k, 1)

    def receive(k, gaps):
        pieces = [2 * gap + part for gap in gaps for part in range(2)]
        for index, piece in enumerate(pieces):
            bin_copy(k, piece).wait()
            pass_on(k, piece)
            if index:
                relay(k, pieces[index - 1])
        relay(k, pieces[-1])

    @pl.loop(0, owned + 1)
    def _(turn_index):
        @pl.when(turn_index < owned)
        def _():
            receive(turn_index, range(1, modules))

        @pl.when(turn_index >= 1)
        def _():
            correlate(turn_index - 1)

    @pl.when(me < 2)
    def _():
        out[:, 0] = jnp.zeros_like(out[:, 0])

    @pl.when(me < 1)
    def _():
        out[:, 1] = jnp.zeros_like(out[:, 1])

    @pl.when(me + 1 >= blocks)
    def _():
        out[:, 3] = jnp.zeros_like(out[:, 3])

    @pl.when(me + 2 >= blocks)
    def _():
        out[:, 4] = jnp.zeros_like(out[:, 4])

    @pl.loop(0, owned)
    def _(k):
        @pl.when(even & has_down)
        def _():
            result_copy(k, 1, 0, me).wait_recv()
            result_copy(k, 2, 1, me).wait_recv()

        @pl.when(odd)
        def _():
            for j in range(parts):
                mate_copy(k, j).wait_send()
            result_copy(k, 0, 1, me).wait_recv()

        @pl.when(sends_far)
        def _():
            for j in range(parts):
                far_copy(k, j).wait_send()

        @pl.when(odd & has_up)
        def _():
            result_copy(k, 3, 3, me).wait_recv()
            result_copy(k, 0, 4, me).wait_recv()

        if relayed:
            @pl.when(relaying & (lax.rem(k, 2) == relay_parity))
            def _():
                for j in range(parts):
                    exit_copy(k, j).wait_send()

        @pl.when(even)
        def _():
            result_copy(k, 0, 1, me + 1).wait_send()

        @pl.when(even & has_up)
        def _():
            result_copy(k, 1, 0, me + 2).wait_send()
            result_copy(k, 2, 1, me + 2).wait_send()
            result_copy(k, 3, 3, me + 1).wait_send()

        @pl.when(odd & has_down)
        def _():
            result_copy(k, 0, 4, me - 2).wait_send()


def correlate(order, turned, sums):
    (pixels, frames), bins = turned.shape, sums.shape[0]
    per_bin = pixels // bins
    blocks, modules = lax.axis_size("frame"), lax.axis_size("module")
    owned = bins // modules
    gathered = per_bin * modules
    vmem = pl.BlockSpec(memory_space=pltpu.VMEM)
    dma = pltpu.SemaphoreType.DMA
    return pl.pallas_call(
        functools.partial(correlate_kernel, blocks, modules),
        out_shape=jax.ShapeDtypeStruct((owned, 5, frames, frames), jnp.float32),
        in_specs=[pl.BlockSpec(memory_space=pltpu.SMEM), vmem, vmem],
        out_specs=vmem,
        scratch_shapes=[
            pltpu.VMEM((modules, bins, frames), jnp.float32),
            pltpu.VMEM((bins, per_bin, frames), jnp.bfloat16),
            pltpu.VMEM((owned, gathered, frames), jnp.bfloat16),
            pltpu.VMEM((owned, gathered, frames), jnp.bfloat16),
            pltpu.VMEM((owned, gathered, frames), jnp.bfloat16),
            pltpu.VMEM((owned, gathered, frames), jnp.bfloat16),
            pltpu.VMEM((4, owned, frames, frames), jnp.float32),
            dma((modules - 1,)),
            dma((modules - 1,)),
            dma((owned, 2 * modules)),
            dma((owned, 2 * modules)),
            dma((2, owned, 2 * modules)),
            dma((2, owned, 2 * modules)),
            dma((owned, 2 * modules)),
            dma((owned, 2 * modules)),
            dma((4, owned)),
            dma((5, owned)),
        ],
        compiler_params=pltpu.CompilerParams(
            collective_id=0, has_side_effects=True, vmem_limit_bytes=VMEM_BYTES
        ),
    )(order, turned, sums)


def per_device(raw_frames, dark_frame, flat_field, membership):
    bins, pixels = membership.shape
    labels = jnp.sum(membership * jnp.arange(bins, dtype=jnp.int32)[:, None], axis=0)
    place = jnp.arange(pixels, dtype=jnp.int32)
    keys = jnp.sort(labels * pixels + place)
    order = keys - place // (pixels // bins) * pixels
    turned, sums = turn(raw_frames, dark_frame, flat_field, membership)
    return correlate(order, turned, sums)[:, None]


def solution(mesh):
    in_specs = (P("frame", "module"), P("module"), P("module"), P(None, "module"))
    out_specs = P("module", "frame", None, None, None)
    return jax.shard_map(
        per_device, mesh=mesh, in_specs=in_specs, out_specs=out_specs, check_vma=False
    )
```
